32 devices in a mesh: dp: 8 (over y, x, core), mp: 4 (over z).
Axes of the slice: x: 2, y: 2, z: 4, core: 2. Of those that a mesh axis runs over, the one named last changes fastest.
Arguments:
- tokens: bfloat16 [64, 256, 1024], P(('dp', 'mp')), may hold values from -6 to 6
- cotangent: bfloat16 [64, 256, 1024], P(('dp', 'mp')), may hold values from -6 to 6
- w_qkv: bfloat16 [3, 1024, 1024], P(None, None, 'mp'), may hold values from -0.1875 to 0.1875
- w_out: bfloat16 [1024, 1024], P('mp'), may hold values from -1 to 1
- w_up: bfloat16 [1024, 4096], P(None, 'mp'), may hold values from -0.1875 to 0.1875
- w_down: bfloat16 [4096, 1024], P('mp'), may hold values from -0.09375 to 0.09375
- w_mod: bfloat16 [1024, 6144], P('mp'), may hold values from -0.1875 to 0.1875
- b_mod: bfloat16 [6, 1024], replicated, may hold values from -3 to 3
- time_weight: bfloat16 [256, 1024], P(None, 'mp'), may hold values from -0.375 to 0.375
- class_table: bfloat16 [1000, 1024], P(None, 'mp'), may hold values from -6 to 6
- rel_table: bfloat16 [16, 961], P('mp'), may hold values from -5 to 5
- window_step: int32 [64], P('dp'), may hold values from 0 to 999
- window_label: int32 [64], P('dp'), may hold values from 0 to 999
- window_cols: int32 [64], P('dp'), may hold values from 0 to 16, as said below
Outputs:
- block_out: bfloat16 [64, 256, 1024], P(('dp', 'mp'))
- tokens_grad: bfloat16 [64, 256, 1024], P(('dp', 'mp'))
- w_qkv_grad: float32 [3, 1024, 1024], P(None, None, 'mp')
- w_out_grad: float32 [1024, 1024], P('mp')
- w_up_grad: float32 [1024, 4096], P(None, 'mp')
- w_down_grad: float32 [4096, 1024], P('mp')
- w_mod_grad: float32 [1024, 6144], P('mp')
- b_mod_grad: float32 [6, 1024], replicated
- time_weight_grad: float32 [256, 1024], P(None, 'mp')
- class_table_grad: float32 [1000, 1024], P(None, 'mp')
- rel_table_grad: float32 [16, 961], P('mp')
The draws below stay inside these ranges and needn't reach their ends.
Inputs may be any that keep to these rules, and one draw needn't show every extreme that they name: `window_cols`: within each aligned block of 8 windows the used slots (nonzero entry) come first, two or more of them; some block is used in full. A used slot holds 16 or 8 valid columns, an unused one 0.
All inputs are finite; a program needn't handle non-finite values.
Results may differ from the reference program's by a relative error of at most 0.028.
Values may be sent and summed in bfloat16 or wider, within the bound.
No kernel may reach another device: no remote copies, remote signals or barrier semaphores. Data moves between devices by JAX's collectives and lax.ppermute only.
A program may use at most 192 MiB of HBM per device.

```python
import math
import jax
import jax.numpy as jnp
from jax import lax

D = 1024
HEADS = 16
FF = 4096
HEAD_DIM = 64
WSIDE = 16
WTOK = 256
RSPAN = 31
FREQ = 256
CLASSES = 1000
WIN_DEV = 8
WINDOWS = 64


def draw_window_cols(key, part):
    keys = jax.random.split(jax.random.fold_in(key, 11), 3)
    blocks = WINDOWS // WIN_DEV
    used_count = jax.random.randint(keys[0], (blocks,), 2, WIN_DEV + 1)
    full_block = jax.random.randint(keys[1], (), 0, blocks)
    used_count = jnp.where(jnp.arange(blocks) == full_block, WIN_DEV, used_count)
    halves = jax.random.randint(keys[2], (blocks, WIN_DEV), 0, 4) == 0
    widths = jnp.where(halves, WSIDE // 2, WSIDE)
    slot_ids = jnp.arange(WIN_DEV)
    widths = jnp.where(slot_ids[None, :] < used_count[:, None], widths, 0)
    return widths.reshape(WINDOWS).astype(jnp.int32)


def plant(values, rng, least, largest):
    spot = [jax.random.randint(jax.random.fold_in(rng, axis), (), 0, length) for axis, length in enumerate(values.shape)]
    main_axis = values.shape.index(max(values.shape))
    neighbour = spot[:main_axis] + [(spot[main_axis] + 1) % values.shape[main_axis]] + spot[main_axis + 1:]
    return values.at[tuple(spot)].set(least).at[tuple(neighbour)].set(largest)


def block_scale(own_key, shape, cuts, smallest, largest):
    loudness, own = 1.0, jax.random.fold_in(own_key, 6)
    for dim, parts in cuts:
        draws = jnp.exp(jax.random.uniform(jax.random.fold_in(own, dim), (parts,), jnp.float32, smallest / len(cuts), largest / len(cuts)))
        loudness = loudness * jnp.repeat(draws, shape[dim] // parts).reshape([-1 if axis == dim else 1 for axis in range(len(shape))])
    return loudness


def centred(rng, dims, scale, most, shards=(), kind=jnp.bfloat16):
    gain = block_scale(rng, dims, shards, -0.22, 0.18) if shards else 1.0
    values = jax.random.normal(rng, dims, jnp.float32) * scale * gain
    return jnp.minimum(jnp.maximum(values, -most), most).astype(kind)


def setup_inputs(seed: int = 0) -> dict:
    key_list = jax.random.split(jax.random.key(seed), 15)
    tokens = centred(key_list[0], (WINDOWS, WTOK, D), 1.0, 6.0, ((0, 32),))
    cotangent = centred(key_list[1], (WINDOWS, WTOK, D), 1.0, 6.0, ((0, 32),))
    w_qkv = centred(key_list[2], (3, D, D), D ** -0.5, 0.1875, ((2, 4),))
    w_out = centred(key_list[3], (D, D), (D // 32) ** -0.5, 1.0, ((0, 4),))
    w_up = centred(key_list[4], (D, FF), D ** -0.5, 0.1875, ((1, 4),))
    w_down = centred(key_list[5], (FF, D), FF ** -0.5, 0.09375, ((0, 4),))
    w_mod = centred(key_list[6], (D, 6 * D), D ** -0.5, 0.1875, ((0, 4),))
    b_mod = centred(key_list[7], (6, D), 0.5, 3.0)
    time_weight = centred(key_list[8], (FREQ, D), FREQ ** -0.5, 0.375, ((1, 4),))
    class_table = centred(key_list[9], (CLASSES, D), 1.0, 6.0, ((1, 4),))
    rel_table = centred(key_list[10], (HEADS, RSPAN * RSPAN), 0.8, 5.0, ((0, 4),))
    window_step = plant(jax.random.randint(key_list[11], (WINDOWS,), 0, 1000), jax.random.fold_in(key_list[11], 1), 0, 999).astype(jnp.int32)
    window_label = plant(jax.random.randint(key_list[12], (WINDOWS,), 0, CLASSES), jax.random.fold_in(key_list[12], 1), 0, CLASSES - 1).astype(jnp.int32)
    window_cols = draw_window_cols(jax.random.fold_in(key_list[14], 71), 0)
    return dict(tokens=tokens, cotangent=cotangent, w_qkv=w_qkv, w_out=w_out, w_up=w_up, w_down=w_down, w_mod=w_mod, b_mod=b_mod, time_weight=time_weight, class_table=class_table, rel_table=rel_table, window_step=window_step, window_label=window_label, window_cols=window_cols)


@jax.custom_vjp
def low(v):
    return lax.optimization_barrier(v.astype(jnp.bfloat16)).astype(jnp.float32)

@jax.custom_vjp
def low_back(v):
    return v

def low_keep(v):
    return (low(v), None)

def low_pass(kept, grad):
    return (grad,)

def back_keep(v):
    return (v, None)

def back_low(kept, grad):
    return (low(grad),)
low.defvjp(low_keep, low_pass)
low_back.defvjp(back_keep, back_low)
EPS = 1e-06
HIGH = lax.Precision.HIGHEST
MASKED = -1000000000.0

def layer_norm(field):
    center = field - lax.optimization_barrier(jnp.mean(field, axis=-1, keepdims=True))
    spread = lax.optimization_barrier(jnp.mean(center * center, axis=-1, keepdims=True))
    return center * lax.rsqrt(spread + EPS)

def modulate(field, scale_part, shift_part):
    return layer_norm(field) * (1.0 + scale_part) + shift_part

def gelu_tanh(field):
    return jax.nn.gelu(field, approximate=True)

def step_features(step_ids, half_width):
    frequency = jnp.exp(-math.log(10000.0) * jnp.arange(half_width, dtype=jnp.float32) / half_width)
    angles = step_ids.astype(jnp.float32)[:, None] * frequency[None, :]
    return jnp.concatenate([jnp.cos(angles), jnp.sin(angles)], axis=1)

def rel_index(window_side):
    position = jnp.arange(window_side * window_side, dtype=jnp.int32)
    row_pos = position // window_side
    col_pos = position % window_side
    row_diff = row_pos[:, None] - row_pos[None, :] + window_side - 1
    col_diff = col_pos[:, None] - col_pos[None, :] + window_side - 1
    return (row_diff * (2 * window_side - 1) + col_diff).astype(jnp.int32)

def window_group(weights, block_in, window_widths, modulation):
    w_qkv, w_out, w_up, w_down, rel_table = weights
    group = block_in.shape[0]
    shift_attn, scale_attn, gate_attn, shift_mlp, scale_mlp, gate_mlp = [modulation[:, column][:, None, :] for column in range(6)]
    keep_keys = (jnp.arange(WTOK, dtype=jnp.int32) % WSIDE)[None, :] < window_widths[:, None]
    normed = low(modulate(block_in, scale_attn, shift_attn))
    heads_shape = (group, WTOK, HEADS, HEAD_DIM)
    queries, keys, values = [low_back(low(jnp.einsum('wtd,de->wte', normed, w_qkv[column], precision=HIGH))).reshape(heads_shape) for column in range(3)]
    rel_bias = rel_table[:, rel_index(WSIDE)]
    scores = jnp.einsum('wihd,wjhd->whij', queries, keys, precision=HIGH) * HEAD_DIM ** (-0.5) + rel_bias[None]
    scores = low_back(jnp.where(keep_keys[:, None, None, :], scores, MASKED))
    probs = jax.nn.softmax(scores, axis=-1)
    attended = low_back(low(jnp.einsum('whij,wjhd->wihd', low(probs), values, precision=HIGH))).reshape(group, WTOK, D)
    branch = low_back(jnp.einsum('wte,ed->wtd', attended, w_out, precision=HIGH))
    middle = block_in + gate_attn * branch
    normed_mlp = low(modulate(middle, scale_mlp, shift_mlp))
    hidden_pre = low_back(jnp.einsum('wtd,df->wtf', normed_mlp, w_up, precision=HIGH))
    activation = low(gelu_tanh(hidden_pre))
    mlp_out = low_back(jnp.einsum('wtf,fd->wtd', activation, w_down, precision=HIGH))
    return jnp.where(keep_keys[:, :, None], middle + gate_mlp * mlp_out, 0.0)

def reference(tokens, cotangent, w_qkv, w_out, w_up, w_down, w_mod, b_mod, time_weight, class_table, rel_table, window_step, window_label, window_cols):
    features = low(step_features(window_step, FREQ // 2))
    group = math.gcd(WINDOWS, 16)
    count_groups = WINDOWS // group

    def forward(block_in, w_qkv, w_out, w_up, w_down, w_mod, b_mod, time_weight, class_table, rel_table):
        cond_pre = jnp.dot(features, time_weight, precision=HIGH, preferred_element_type=jnp.float32) + class_table[window_label]
        condition = low(jax.nn.silu(cond_pre))
        modulation = jnp.dot(condition, w_mod, precision=HIGH, preferred_element_type=jnp.float32).reshape(WINDOWS, 6, D) + b_mod[None]
        weights = (w_qkv, w_out, w_up, w_down, rel_table)

        def run_group(piece):
            return window_group(weights, piece[0], piece[1], piece[2])
        result = lax.map(jax.checkpoint(run_group), (block_in.reshape(count_groups, group, WTOK, D), window_cols.reshape(count_groups, group), modulation.reshape(count_groups, group, 6, D)))
        return result.reshape(WINDOWS, WTOK, D)
    floats = [array.astype(jnp.float32) for array in (tokens, w_qkv, w_out, w_up, w_down, w_mod, b_mod, time_weight, class_table, rel_table)]
    result, pull = jax.vjp(forward, *floats)
    grads = pull(cotangent.astype(jnp.float32))
    return (result.astype(jnp.bfloat16), grads[0].astype(jnp.bfloat16), grads[1], grads[2], grads[3], grads[4], grads[5], grads[6], grads[7], grads[8], grads[9])
```

```python
import functools
import math

import jax
import jax.numpy as jnp
from jax import lax
from jax.experimental import pallas as pl
from jax.experimental.pallas import tpu as pltpu
from jax.sharding import PartitionSpec as P

HEAD_DIM = 64
WSIDE = 16
FREQ = 256
EPS = 1e-06
HIGH = lax.Precision.HIGHEST
MASKED = -1000000000.0
F32 = jnp.float32
BF16 = jnp.bfloat16
SHIFT_ATTN, SCALE_ATTN, GATE_ATTN, SHIFT_MLP, SCALE_MLP, GATE_MLP = range(6)
SMEM = pl.BlockSpec(memory_space=pltpu.SMEM)


def mm(a, b):
    return jnp.dot(a, b, preferred_element_type=F32)


def mm_nt(a, b):
    return lax.dot_general(a, b, (((1,), (1,)), ((), ())), preferred_element_type=F32)


def mm_tn(a, b):
    return lax.dot_general(a, b, (((0,), (0,)), ((), ())), preferred_element_type=F32)


def norm_parts(field):
    center = field - jnp.mean(field, axis=-1, keepdims=True)
    inverse = lax.rsqrt(jnp.mean(center * center, axis=-1, keepdims=True) + EPS)
    return center * inverse, inverse


def norm_back(hat, inverse, grad):
    mean_grad = jnp.mean(grad, axis=-1, keepdims=True)
    mean_hat = jnp.mean(grad * hat, axis=-1, keepdims=True)
    return (grad - mean_grad - hat * mean_hat) * inverse


def row_keep(cols, shape):
    return lax.broadcasted_iota(jnp.int32, shape, 0) % WSIDE < cols


def whole(*shape):
    return pl.BlockSpec(shape, lambda *_: (0,) * len(shape))


def cost(flops, moved, trans=0):
    return pl.CostEstimate(flops=int(flops), bytes_accessed=int(moved), transcendentals=int(trans))


def call(body, name, grid, ins, outs, shapes, flops, moved, scratch=()):
    return pl.pallas_call(
        body,
        name=name,
        grid=grid,
        in_specs=ins,
        out_specs=outs,
        out_shape=shapes,
        scratch_shapes=scratch,
        compiler_params=pltpu.CompilerParams(vmem_limit_bytes=60 * 2**20),
        cost_estimate=cost(flops, moved),
    )


def qkv_body(count, x_ref, mod_ref, w_ref, normed_ref, out_ref):
    rows = x_ref.shape[0] // count

    @pl.when((pl.program_id(0) == 0) & (pl.program_id(1) == 0))
    def _():
        for win in range(count):
            part = pl.ds(win * rows, rows)
            hat, _ = norm_parts(x_ref[part, :].astype(F32))
            normed_ref[part, :] = (
                hat * (1.0 + mod_ref[win, SCALE_ATTN, :][None]) + mod_ref[win, SHIFT_ATTN, :][None]
            ).astype(BF16)

    out_ref[0] = mm(normed_ref[...], w_ref[0, 0]).astype(BF16)


def offset_lanes(width, span):
    lane = lax.broadcasted_iota(jnp.int32, (width, 2 * width), 1)
    row = lax.broadcasted_iota(jnp.int32, (width, 2 * width), 0)
    return lane, row, span


def expand_bias(table, pick):
    lanes = pick.shape[1]
    spread = mm(table, pick)
    col = lax.broadcasted_iota(jnp.int32, (WSIDE, lanes), 1) % WSIDE
    grid = jnp.zeros((WSIDE, lanes), F32)
    for step in range(WSIDE):
        low = WSIDE - 1 - step
        grid = jnp.where(col == step, spread[low : low + WSIDE, :], grid)
    return jnp.concatenate(
        [
            grid[:, (WSIDE - 1 - row) * WSIDE : (2 * WSIDE - 1 - row) * WSIDE]
            for row in range(WSIDE)
        ],
        axis=0,
    )


def score_parts(query, key, bias, keep):
    raw = mm_nt(query, key) * HEAD_DIM**-0.5 + bias
    raw = jnp.where(keep, raw, MASKED)
    power = jnp.exp(raw - jnp.max(raw, axis=-1, keepdims=True))
    return power / jnp.sum(power, axis=-1, keepdims=True)


def attn_fwd_body(count, cols_ref, qkv_ref, table_ref, pick_ref, out_ref):
    rows = out_ref.shape[1] // count
    lane = lax.broadcasted_iota(jnp.int32, (1, rows), 1) % WSIDE
    for head in range(2):
        bias = expand_bias(table_ref[head], pick_ref[...])
        feat = pl.ds(head * HEAD_DIM, HEAD_DIM)
        for win in range(count):
            part = pl.ds(win * rows, rows)
            probs = score_parts(
                qkv_ref[0, part, feat], qkv_ref[1, part, feat], bias, lane < cols_ref[win]
            )
            out_ref[0, part, feat] = mm(probs.astype(BF16), qkv_ref[2, part, feat]).astype(BF16)


def attn_bwd_body(count, cols_ref, qkv_ref, dout_ref, table_ref, pick_ref, d_ref, dtab_ref, acc):
    rows = dout_ref.shape[0] // count
    lane = lax.broadcasted_iota(jnp.int32, (1, rows), 1) % WSIDE
    lanes = pick_ref.shape[1]
    col = lax.broadcasted_iota(jnp.int32, (WSIDE, lanes), 1) % WSIDE
    scale = HEAD_DIM**-0.5
    pair = 2 * HEAD_DIM
    for head in range(2):
        bias = expand_bias(table_ref[head], pick_ref[...])
        feat = pl.ds(head * HEAD_DIM, HEAD_DIM)
        total = jnp.zeros((rows, rows), F32)
        for win in range(count):
            part = pl.ds(win * rows, rows)
            query, key, value = (qkv_ref[k, part, feat] for k in range(3))
            dout = dout_ref[part, feat]
            probs = score_parts(query, key, bias, lane < cols_ref[win])
            d_probs = mm_nt(dout, value)
            d_ref[0, part, pl.ds(2 * pair + head * HEAD_DIM, HEAD_DIM)] = mm_tn(probs.astype(BF16), dout).astype(BF16)
            delta = jnp.sum(probs * d_probs, axis=-1, keepdims=True)
            d_scores = (probs * (d_probs - delta)).astype(BF16)
            d_ref[0, part, pl.ds(0 * pair + head * HEAD_DIM, HEAD_DIM)] = (mm(d_scores, key) * scale).astype(BF16)
            d_ref[0, part, pl.ds(1 * pair + head * HEAD_DIM, HEAD_DIM)] = (mm_tn(d_scores, query) * scale).astype(BF16)
            total = total + d_scores.astype(F32)
        grid = jnp.zeros((WSIDE, lanes), F32)
        pad = jnp.zeros((WSIDE, lanes - rows), F32)
        for row in range(WSIDE):
            block = jnp.concatenate([total[row * WSIDE : (row + 1) * WSIDE, :], pad], axis=1)
            offset = (WSIDE - 1 - row) * WSIDE
            grid = grid + (pltpu.roll(block, offset, 1) if offset else block)
        acc[...] = jnp.zeros_like(acc)
        for step in range(WSIDE):
            low = WSIDE - 1 - step
            acc[low : low + WSIDE, :] += jnp.where(col == step, grid, 0.0)
        dtab_ref[head] = lax.dot_general(
            acc[...],
            pick_ref[...].astype(F32),
            (((1,), (1,)), ((), ())),
            precision=HIGH,
            preferred_element_type=F32,
        )


def out_proj_body(x_ref, att_ref, w_ref, mod_ref, mid_ref, branch_ref, normed_ref):
    branch = sum(
        mm(att_ref[side], w_ref[:, side].reshape(att_ref.shape[2], w_ref.shape[3]))
        for side in range(2)
    )
    middle = x_ref[...].astype(F32) + mod_ref[0, GATE_ATTN, :][None] * branch
    hat, _ = norm_parts(middle)
    mid_ref[...] = middle
    branch_ref[...] = branch.astype(BF16)
    normed_ref[...] = (
        hat * (1.0 + mod_ref[0, SCALE_MLP, :][None]) + mod_ref[0, SHIFT_MLP, :][None]
    ).astype(BF16)


def up_body(n_ref, w_ref, act_ref, slope_ref):
    value = mm(n_ref[...], w_ref[0])
    root = math.sqrt(2.0 / math.pi)
    square = value * value
    bent = jnp.tanh(root * (value + 0.044715 * square * value))
    half = 0.5 * (1.0 + bent)
    act_ref[0] = (value * half).astype(BF16)
    slope_ref[0] = (
        half + 0.5 * value * (1.0 - bent * bent) * (root * (1.0 + 3 * 0.044715 * square))
    ).astype(BF16)


def down_body(count, cols_ref, act_ref, w_ref, mid_ref, cot_ref, mod_ref, out_ref, dgate_ref):
    mlp_out = sum(
        mm(act_ref[side], w_ref[:, side].reshape(act_ref.shape[2], w_ref.shape[3]))
        for side in range(2)
    )
    rows = out_ref.shape[0] // count
    for win in range(count):
        part = slice(win * rows, (win + 1) * rows)
        keep = row_keep(cols_ref[win], (rows, 1))
        mine = mlp_out[part]
        out_ref[part, :] = jnp.where(
            keep, mid_ref[part, :] + mod_ref[win, GATE_MLP, :][None] * mine, 0.0
        ).astype(BF16)
        grad = jnp.where(keep, cot_ref[part, :].astype(F32), 0.0)
        dgate_ref[win, :] = jnp.sum(grad * mine, axis=0)


def dact_body(d_ref, w_ref, slope_ref, out_ref):
    out_ref[0] = (mm_nt(d_ref[...], w_ref[...]) * slope_ref[0].astype(F32)).astype(BF16)


def dnorm_mlp_body(
    count, cols_ref, dh_ref, w_ref, mid_ref, cot_ref, branch_ref, mod_ref,
    dmid_ref, dbranch_ref, sums_ref, acc,
):
    step = pl.program_id(0)
    half = dh_ref.shape[2]
    piece = mm_nt(dh_ref[0], w_ref[0, :, :half]) + mm_nt(dh_ref[1], w_ref[0, :, half:])

    @pl.when(step == 0)
    def _():
        acc[...] = piece

    @pl.when(step > 0)
    def _():
        acc[...] += piece

    @pl.when(step == pl.num_programs(0) - 1)
    def _():
        rows = mid_ref.shape[0] // count
        for win in range(count):
            part = pl.ds(win * rows, rows)
            upper = acc[part, :]
            hat, inverse = norm_parts(mid_ref[part, :])
            keep = row_keep(cols_ref[win], (rows, 1))
            d_middle = jnp.where(keep, cot_ref[part, :].astype(F32), 0.0) + norm_back(
                hat, inverse, upper * (1.0 + mod_ref[win, SCALE_MLP, :][None])
            )
            dmid_ref[part, :] = d_middle
            dbranch_ref[part, :] = (mod_ref[win, GATE_ATTN, :][None] * d_middle).astype(BF16)
            sums_ref[win, 0, :] = jnp.sum(d_middle * branch_ref[part, :].astype(F32), axis=0)
            sums_ref[win, 1, :] = jnp.sum(upper, axis=0)
            sums_ref[win, 2, :] = jnp.sum(upper * hat, axis=0)


def datt_body(d_ref, w_ref, out_ref):
    out_ref[...] = mm_nt(d_ref[...], w_ref[...]).astype(BF16)


def dnorm_attn_body(count, d_ref, w_ref, x_ref, dmid_ref, mod_ref, out_ref, sums_ref, acc):
    step = pl.program_id(0)
    first = step == 0
    last = step == pl.num_programs(0) - 1
    pair = 2 * HEAD_DIM
    piece = sum(
        mm_nt(
            jnp.concatenate([d_ref[side, :, k * pair : (k + 1) * pair] for side in range(2)], axis=1),
            w_ref[0, k],
        )
        for k in range(3)
    )

    @pl.when(first)
    def _():
        acc[...] = piece

    @pl.when(jnp.logical_not(first))
    def _():
        acc[...] += piece

    @pl.when(last)
    def _():
        rows = x_ref.shape[0] // count
        for win in range(count):
            part = pl.ds(win * rows, rows)
            upper = acc[part, :]
            hat, inverse = norm_parts(x_ref[part, :].astype(F32))
            out_ref[part, :] = (
                dmid_ref[part, :]
                + norm_back(hat, inverse, upper * (1.0 + mod_ref[win, SCALE_ATTN, :][None]))
            ).astype(BF16)
            sums_ref[win, 0, :] = jnp.sum(upper, axis=0)
            sums_ref[win, 1, :] = jnp.sum(upper * hat, axis=0)


def spread_grad(result, place, quarter, slot, refs):
    send_a, keep_a, send_b, keep_b = refs
    size = result.shape[0] // 4
    for index in range(4):
        piece = result[index * size : (index + 1) * size].astype(BF16)
        other = quarter ^ index
        down, right = other // 2, other % 2

        @pl.when((slot < 2) & (right == 1))
        def _():
            send_a[down, slot] = piece

        @pl.when((slot < 2) & (right == 0))
        def _():
            keep_a[down, slot] = piece

        @pl.when((slot >= 2) & (down == 1))
        def _():
            send_b[right, slot - 2] = piece

        @pl.when((slot >= 2) & (down == 0))
        def _():
            keep_b[right, slot - 2] = piece


def grad_body(parts, place_ref, x0_ref, x1_ref, y0_ref, y1_ref, *refs):
    shape = lambda ref: ref[...].reshape(ref.shape[-2:])
    result = mm_tn(shape(x0_ref), shape(y0_ref)) + mm_tn(shape(x1_ref), shape(y1_ref))
    slot = (pl.program_id(0) + parts - place_ref[0]) % parts
    spread_grad(result, place_ref[0], place_ref[1], slot, refs)


def grad_out_body(parts, place_ref, x0_ref, x1_ref, y0_ref, y1_ref, *refs):
    result = mm_tn(x0_ref[...], y0_ref[...]) + mm_tn(x1_ref[...], y1_ref[...])
    size = result.shape[0] // parts
    for index in range(parts):
        slot = (index + parts - place_ref[0]) % parts
        spread_grad(result[index * size : (index + 1) * size], place_ref[0], place_ref[1], slot, refs)


def join_body(copies, place_ref, own_ref, *refs):
    out_ref = refs[-1]
    step = pl.program_id(0)
    mine = place_ref[2] * (copies // 2) + place_ref[1]
    size = own_ref.shape[0] // copies

    @pl.when(step == 0)
    def _():
        out_ref[0] = own_ref[...]

    @pl.when(step > 0)
    def _():
        for core in range(2):
            for index, ref in enumerate(refs[5 * core : 5 * core + 5]):
                which = mine ^ (core * (copies // 2) + min(index, 3))
                length = ref.shape[1]
                start = which * size + (size // 2 if index == 4 else 0)
                out_ref[0, pl.ds(pl.multiple_of(start, size // 2), length), :] = ref[0]


def finish_body(split, kinds, place_ref, near_ref, far_ref, out_ref):
    rows, cols = near_ref.shape[1:]
    for core in range(2):
        side = place_ref[2] ^ core
        for index in range(4):
            quarter = place_ref[1] ^ index
            piece = (near_ref, far_ref)[core][index].astype(F32)
            if split == "rows":
                start = pl.multiple_of((side * 4 + quarter) * rows, rows)
                out_ref[pl.ds(start, rows), :] = piece
            else:
                start = pl.multiple_of(quarter * rows, rows)
                width = cols // kinds
                for kind in range(kinds):
                    out_ref[
                        kind, pl.ds(start, rows), pl.ds(pl.multiple_of(side * width, width), width)
                    ] = piece[:, kind * width : (kind + 1) * width]


def step_features(step_ids, half_width):
    frequency = jnp.exp(-math.log(10000.0) * jnp.arange(half_width, dtype=F32) / half_width)
    angles = step_ids.astype(F32)[:, None] * frequency[None, :]
    return jnp.concatenate([jnp.cos(angles), jnp.sin(angles)], axis=1)


def per_device(
    mesh, tokens, cotangent, w_qkv, w_out, w_up, w_down, w_mod, b_mod, time_weight, class_table,
    rel_table, window_step, window_label, window_cols,
):
    count, win_tok, width = tokens.shape
    rows = count * win_tok
    group = window_step.shape[0]
    parts, copies = mesh.shape["mp"], mesh.shape["dp"]
    direct = parts == 4 and copies == 8
    shard = w_qkv.shape[2]
    hidden = w_up.shape[1]
    half, wide, pair = hidden // 2, parts * hidden, 2 * HEAD_DIM
    heads = parts * shard // HEAD_DIM
    local_heads = rel_table.shape[0]
    span = 2 * WSIDE - 1
    my_copy, my_part = lax.axis_index("dp"), lax.axis_index("mp")
    core, quarter = my_copy % 2, my_copy // 2
    place = jnp.stack([my_part, quarter, core]).astype(jnp.int32)
    first_own = my_part * count
    f32s, bf16s = (functools.partial(jax.ShapeDtypeStruct, dtype=kind) for kind in (F32, BF16))

    def hop(value, bits):
        return lax.ppermute(value, "dp", [(i, i ^ bits) for i in range(copies)])

    def turn(value, step):
        return lax.ppermute(value, "mp", [(i, (i + step) % parts) for i in range(parts)])

    def placed(body, name, grid, ins, outs, shapes, flops, moved):
        return pl.pallas_call(
            body,
            name=name,
            grid_spec=pltpu.PrefetchScalarGridSpec(
                num_scalar_prefetch=1, grid=grid, in_specs=ins, out_specs=outs
            ),
            out_shape=shapes,
            compiler_params=pltpu.CompilerParams(vmem_limit_bytes=60 * 2**20),
            cost_estimate=cost(flops, moved),
        )

    def gather_weight(weight):
        total, cols = weight.shape
        size = total // copies
        if not direct:
            piece = lax.dynamic_slice_in_dim(weight, my_copy * size, size, 0)
            whole_weight = lax.all_gather(piece, ("mp", "dp"), axis=0, tiled=True)
            return whole_weight.reshape(parts, total, cols)
        piece = lax.dynamic_slice_in_dim(weight, (core * 4 + quarter) * size, size, 0)
        mine = jnp.stack([turn(piece, step) for step in range(1, parts)])
        right, down = hop(mine, 2), hop(mine, 4)
        cut = size // 2
        near = [mine, right, down, hop(right[:, :cut], 4), hop(down[:, cut:], 2)]
        far = [hop(value, 1) for value in near]
        return placed(
            functools.partial(join_body, copies), "join", (parts,),
            [whole(total, cols)] + [
                pl.BlockSpec(
                    (1,) + value.shape[1:], lambda s, p: (jnp.maximum(s - 1, 0), 0, 0)
                )
                for value in near + far
            ],
            pl.BlockSpec((1, total, cols), lambda s, p: ((p[0] + parts - s) % parts, 0, 0)),
            bf16s((parts, total, cols)), 0, 4 * parts * total * cols,
        )(place, weight, *near, *far)

    def finish_grad(parts_of, split, kinds, out_shape):
        send_a, keep_a, send_b, keep_b = parts_of
        wide_of = lambda value: value.astype(F32)
        got_a, got_b = hop(send_a, 2), hop(send_b, 4)
        next_a = hop((wide_of(keep_a[1]) + wide_of(got_a[1])).astype(BF16), 4)
        next_b = hop((wide_of(keep_b[1]) + wide_of(got_b[1])).astype(BF16), 2)
        sum_a = wide_of(keep_a[0]) + wide_of(got_a[0]) + wide_of(next_a)
        sum_b = wide_of(keep_b[0]) + wide_of(got_b[0]) + wide_of(next_b)
        total = (
            sum_a[0]
            + wide_of(turn(sum_a[1].astype(BF16), 1))
            + wide_of(turn(sum_b[0].astype(BF16), 2))
            + wide_of(turn(sum_b[1].astype(BF16), 3))
        ).astype(BF16)
        near = jnp.stack([total, hop(total, 2), hop(total, 4), hop(total, 6)])
        far = hop(near, 1)
        return placed(
            functools.partial(finish_body, split, kinds), "finish", (1,),
            [whole(*near.shape)] * 2, whole(*out_shape), f32s(out_shape), 0,
            4 * near.size + 4 * math.prod(out_shape),
        )(place, near, far)

    def flat_grad(grad):
        piece = lax.psum_scatter(grad.astype(BF16), ("mp", "dp"), scatter_dimension=0, tiled=True)
        return lax.all_gather(piece, "dp", axis=0, tiled=True).astype(F32)

    classes = jnp.arange(class_table.shape[0], dtype=jnp.int32)

    def condition_of(step_ids, labels):
        feats = step_features(step_ids, FREQ // 2).astype(BF16)
        hot = (labels[:, None] == classes[None, :]).astype(BF16)
        return feats, hot, mm(feats, time_weight) + mm(hot, class_table)

    own_condition = jax.nn.silu(condition_of(window_step, window_label)[2]).astype(BF16)
    partial_mod = mm(own_condition, w_mod)
    ids = jnp.stack([window_step, window_label])
    if direct:
        take = lambda step: lax.dynamic_slice_in_dim(
            partial_mod, (my_part + step) % parts * count, count, 0
        )
        mod = take(0) + sum(turn(take(step), step) for step in range(1, parts))
        tables = jnp.zeros((parts, local_heads, rel_table.shape[1]), BF16)
        for step in range(parts):
            got = turn(rel_table, step) if step else rel_table
            tables = lax.dynamic_update_index_in_dim(tables, got, (my_part + parts - step) % parts, 0)
        for bits in (1, 2, 4):
            ids = jnp.concatenate([ids, hop(ids, bits)], axis=1)
    else:
        mod = lax.psum_scatter(partial_mod, "mp", scatter_dimension=0, tiled=True)
        tables = lax.all_gather(rel_table, "mp", axis=0, tiled=True)
        ids = lax.all_gather(ids, "dp", axis=1, tiled=True)
    mod = mod.reshape(count, 6, width) + b_mod.astype(F32)[None]
    own_cols = lax.dynamic_slice_in_dim(window_cols, first_own, count, 0)
    table = tables.reshape(heads, span, span).transpose(0, 2, 1)
    table = jnp.pad(table, ((0, 0), (0, 1), (0, 1)))
    lanes = 2 * win_tok
    pick = (
        jnp.arange(span + 1, dtype=jnp.int32)[:, None]
        == span - 1 - jnp.arange(lanes, dtype=jnp.int32)[None, :] // WSIDE
    ).astype(BF16)

    all_qkv = gather_weight(w_qkv.reshape(3 * width, shard)).reshape(parts, 3, width, shard)
    all_out = gather_weight(w_out).reshape(parts, 2, pair, width)
    all_up = gather_weight(w_up)
    all_down = gather_weight(w_down).reshape(parts, 2, half, width)

    inputs = tokens.reshape(rows, width)
    cot = cotangent.reshape(rows, width)
    keep_rows = (jnp.arange(win_tok, dtype=jnp.int32) % WSIDE)[None, :] < own_cols[:, None]
    d_mlp = (
        mod[:, GATE_MLP][:, None, :] * jnp.where(keep_rows[:, :, None], cotangent.astype(F32), 0.0)
    ).astype(BF16).reshape(rows, width)

    normed_attn, qkv = call(
        functools.partial(qkv_body, count), "qkv", (parts, 3),
        [
            whole(rows, width),
            whole(count, 6, width),
            pl.BlockSpec((1, 1, width, shard), lambda z, k: (z, k, 0, 0)),
        ],
        [whole(rows, width), pl.BlockSpec((1, rows, shard), lambda z, k: (k, 0, z))],
        [bf16s((rows, width)), bf16s((3, rows, width))],
        2 * rows * width * 3 * width, 2 * (3 * width * width + 4 * rows * width),
    )(inputs, mod, all_qkv)

    qkv_spec = pl.BlockSpec((3, rows, pair), lambda i: (0, 0, i))
    pair_spec = pl.BlockSpec((rows, pair), lambda i: (0, i))
    table_spec = pl.BlockSpec((2, span + 1, span + 1), lambda i: (i, 0, 0))
    pick_spec = whole(span + 1, lanes)
    attended = call(
        functools.partial(attn_fwd_body, count), "attn_fwd", (heads // 2,),
        [SMEM, qkv_spec, table_spec, pick_spec],
        pl.BlockSpec((1, rows, pair), lambda i: (i % 2, 0, i // 2)),
        bf16s((2, rows, parts * pair)),
        4 * rows * win_tok * width, 8 * rows * width,
    )(own_cols, qkv, table, pick)

    win_spec = pl.BlockSpec((win_tok, width), lambda w: (w, 0))
    mod_spec = pl.BlockSpec((1, 6, width), lambda w: (w, 0, 0))
    middle, branch, normed_mlp = call(
        out_proj_body, "out_proj", (count,),
        [
            win_spec, pl.BlockSpec((2, win_tok, parts * pair), lambda w: (0, w, 0)),
            whole(parts, 2, pair, width), mod_spec,
        ],
        [win_spec] * 3,
        [f32s((rows, width)), bf16s((rows, width)), bf16s((rows, width))],
        2 * rows * width * width, 2 * width * width + 12 * rows * width,
    )(inputs, attended, all_out, mod)

    half_spec = pl.BlockSpec((1, rows, half), lambda z, j: (j, 0, z))
    activation, slope = call(
        up_body, "up", (parts, 2),
        [whole(rows, width), pl.BlockSpec((1, width, half), lambda z, j: (z, 0, j))],
        [half_spec, half_spec], [bf16s((2, rows, parts * half))] * 2,
        2 * rows * width * wide, 2 * width * wide + 4 * rows * wide,
    )(normed_mlp, all_up)

    def grad_of(name, body, grid, left, right, left_spec, right_spec, shape):
        flops = 4 * rows * left[0].shape[1] * right[0].shape[1]
        moved = 4 * rows * (left[0].shape[1] + right[0].shape[1]) + 32 * shape[0] * shape[1]
        return placed(
            functools.partial(body, parts), name, grid,
            [left_spec, left_spec, right_spec, right_spec],
            [whole(2, 2, *shape)] * 4, [bf16s((2, 2, *shape))] * 4, flops, moved,
        )(place, *left, *right)

    def both(value):
        return value, hop(value, 1)

    def halves(value):
        side = lambda which: lax.dynamic_index_in_dim(value, which, 0, keepdims=False)
        return side(core), hop(side(1 - core), 1)

    full = whole(rows, width)
    slab = lambda size: pl.BlockSpec((rows, size), lambda z, p: (0, z))
    if direct:
        down_parts = grad_of(
            "down_grad", grad_body, (parts,), halves(activation), both(d_mlp), slab(half), full,
            (half // 4, width),
        )

    d_hidden = call(
        dact_body, "dact", (parts, 2),
        [
            whole(rows, width), pl.BlockSpec((half, width), lambda z, j: (2 * z + j, 0)),
            half_spec,
        ],
        half_spec, bf16s((2, rows, parts * half)),
        2 * rows * width * wide, 2 * width * wide + 4 * rows * wide,
    )(d_mlp, all_down.reshape(wide, width), slope)
    if direct:
        up_parts = grad_of(
            "up_grad", grad_body, (parts,), both(normed_mlp), halves(d_hidden), full, slab(half),
            (width // 4, half),
        )

    d_middle, d_branch, sums_mlp = call(
        functools.partial(dnorm_mlp_body, count), "dnorm_mlp", (parts,),
        [
            SMEM, pl.BlockSpec((2, rows, half), lambda z: (0, 0, z)),
            pl.BlockSpec((1, width, hidden), lambda z: (z, 0, 0)),
            whole(rows, width), whole(rows, width), whole(rows, width), whole(count, 6, width),
        ],
        [whole(rows, width), whole(rows, width), whole(count, 3, width)],
        [f32s((rows, width)), bf16s((rows, width)), f32s((count, 3, width))],
        2 * rows * width * wide, 2 * width * wide + 2 * rows * wide + 12 * rows * width,
        scratch=[pltpu.VMEM((rows, width), F32)],
    )(own_cols, d_hidden, all_up, middle, cot, branch, mod)

    if direct:
        out_parts = grad_of(
            "out_grad", grad_out_body, (1,), halves(attended), both(d_branch),
            whole(rows, parts * pair), full, (pair // 4, width),
        )

    d_attended = call(
        datt_body, "datt", (2,),
        [whole(rows, width), pl.BlockSpec((width // 2, width), lambda m: (m, 0))],
        pl.BlockSpec((rows, width // 2), lambda m: (0, m)), bf16s((rows, width)),
        2 * rows * width * width, 2 * width * width + 4 * rows * width,
    )(d_branch, all_out.reshape(width, width))

    d_qkv, d_table = call(
        functools.partial(attn_bwd_body, count), "attn_bwd", (heads // 2,),
        [SMEM, qkv_spec, pair_spec, table_spec, pick_spec],
        [pl.BlockSpec((1, rows, 3 * pair), lambda i: (i % 2, 0, i // 2)), table_spec],
        [bf16s((2, rows, parts * 3 * pair)), f32s((heads, span + 1, span + 1))],
        10 * rows * win_tok * width, 14 * rows * width,
        scratch=[pltpu.VMEM((span + 1, lanes), F32)],
    )(own_cols, qkv, d_attended, table, pick)

    if direct:
        qkv_parts = grad_of(
            "qkv_grad", grad_body, (parts,), both(normed_attn), halves(d_qkv), full,
            slab(3 * pair), (width // 4, 3 * pair),
        )

    tokens_grad, sums_attn = call(
        functools.partial(dnorm_attn_body, count), "dnorm_attn", (parts,),
        [
            pl.BlockSpec((2, rows, 3 * pair), lambda z: (0, 0, z)),
            pl.BlockSpec((1, 3, width, shard), lambda z: (z, 0, 0, 0)),
            whole(rows, width), whole(rows, width), whole(count, 6, width),
        ],
        [whole(rows, width), whole(count, 2, width)],
        [bf16s((rows, width)), f32s((count, 2, width))],
        2 * rows * width * 3 * width, 2 * (3 * width * width + 6 * rows * width),
        scratch=[pltpu.VMEM((rows, width), F32)],
    )(d_qkv, all_qkv, inputs, d_middle, mod)

    lane_block = width // 4
    lane_spec = pl.BlockSpec((rows, lane_block), lambda n: (0, n))
    block_out, d_gate_mlp = call(
        functools.partial(down_body, count), "down", (4,),
        [
            SMEM, whole(2, rows, parts * half),
            pl.BlockSpec((parts, 2, half, lane_block), lambda n: (0, 0, 0, n)),
            lane_spec, lane_spec, pl.BlockSpec((count, 6, lane_block), lambda n: (0, 0, n)),
        ],
        [lane_spec, pl.BlockSpec((count, lane_block), lambda n: (0, n))],
        [bf16s((rows, width)), f32s((count, width))],
        2 * rows * width * wide, 2 * width * wide + 2 * rows * wide,
    )(own_cols, activation, all_down, middle, cot, mod)

    if direct:
        w_down_grad = finish_grad(down_parts, "rows", 1, (hidden, width))
        w_up_grad = finish_grad(up_parts, "cols", 1, (1, width, hidden)).reshape(width, hidden)
        w_out_grad = finish_grad(out_parts, "rows", 1, (shard, width))
        w_qkv_grad = finish_grad(qkv_parts, "cols", 3, (3, width, shard))
    else:
        join = lambda value, size: value.reshape(2, rows, parts, size).transpose(1, 2, 0, 3)
        w_down_grad = flat_grad(mm_tn(join(activation, half).reshape(rows, wide), d_mlp))
        up_flat = mm_tn(normed_mlp, join(d_hidden, half).reshape(rows, wide))
        w_up_grad = flat_grad(
            up_flat.reshape(width, parts, hidden).transpose(1, 0, 2).reshape(parts * width, hidden)
        )
        w_out_grad = flat_grad(mm_tn(join(attended, pair).reshape(rows, width), d_branch))
        d_flat = d_qkv.reshape(2, rows, parts, 3, pair).transpose(1, 2, 3, 0, 4)
        qkv_flat = mm_tn(normed_attn, d_flat.reshape(rows, 3 * width))
        w_qkv_grad = flat_grad(
            qkv_flat.reshape(width, parts * 3, shard).transpose(1, 0, 2).reshape(-1, shard)
        ).reshape(3, width, shard)

    d_mod_own = jnp.concatenate(
        [sums_attn, sums_mlp, d_gate_mlp[:, None, :]], axis=1
    ).reshape(count, 6 * width).astype(BF16)
    if direct:
        own_table = lambda step: lax.dynamic_slice_in_dim(
            d_table, (my_part + step) % parts * local_heads, local_heads, 0
        )
        d_table = own_table(0) + sum(turn(own_table(step), step) for step in range(1, parts))
        for bits in (1, 2, 4):
            d_table = d_table + hop(d_table, bits)
        d_mod = jnp.zeros((group, 6 * width), BF16)
        for step in range(parts):
            got = turn(d_mod_own, step) if step else d_mod_own
            d_mod = lax.dynamic_update_slice_in_dim(
                d_mod, got, (my_part + parts - step) % parts * count, 0
            )
        for bits in (1, 2, 4):
            d_mod = jnp.concatenate([d_mod, hop(d_mod, bits)], axis=0)
    else:
        d_table = lax.psum(d_table, ("dp", "mp"))
        d_table = lax.dynamic_slice_in_dim(d_table, my_part * local_heads, local_heads, 0)
        d_mod = lax.all_gather(d_mod_own, ("dp", "mp"), axis=0, tiled=True)
    rel_table_grad = d_table[:, :span, :span].transpose(0, 2, 1).reshape(local_heads, span * span)
    features, onehot, cond_pre = condition_of(ids[0], ids[1])
    condition = jax.nn.silu(cond_pre).astype(BF16)
    d_condition = lax.dot_general(
        d_mod, w_mod, (((1,), (1,)), ((), ())), preferred_element_type=F32
    )
    d_cond_pre = jax.vjp(jax.nn.silu, cond_pre)[1](d_condition)[0]
    time_weight_grad = lax.dot_general(
        features.astype(F32), d_cond_pre, (((0,), (0,)), ((), ())), precision=HIGH,
        preferred_element_type=F32,
    )
    class_table_grad = lax.dot_general(
        onehot.astype(F32), d_cond_pre, (((0,), (0,)), ((), ())), precision=HIGH,
        preferred_element_type=F32,
    )
    w_mod_grad = mm_tn(condition, d_mod)
    b_mod_grad = jnp.sum(d_mod.astype(F32), axis=0).reshape(6, width)
    return (
        block_out.reshape(tokens.shape), tokens_grad.reshape(tokens.shape), w_qkv_grad, w_out_grad,
        w_up_grad, w_down_grad, w_mod_grad, b_mod_grad, time_weight_grad, class_table_grad,
        rel_table_grad,
    )


def solution(mesh):
    return jax.shard_map(
        functools.partial(per_device, mesh),
        mesh=mesh,
        in_specs=(
            P(("dp", "mp"), None, None),
            P(("dp", "mp"), None, None),
            P(None, None, "mp"),
            P("mp", None),
            P(None, "mp"),
            P("mp", None),
            P("mp", None),
            P(),
            P(None, "mp"),
            P(None, "mp"),
            P("mp", None),
            P("dp"),
            P("dp"),
            P("dp"),
        ),
        out_specs=(
            P(("dp", "mp"), None, None),
            P(("dp", "mp"), None, None),
            P(None, None, "mp"),
            P("mp", None),
            P(None, "mp"),
            P("mp", None),
            P("mp", None),
            P(),
            P(None, "mp"),
            P(None, "mp"),
            P("mp", None),
        ),
        check_vma=False,
    )
```
